32 devices in a mesh: seq: 8 (over z, y), head: 4 (over x, core).
Axes of the slice: x: 2, y: 2, z: 4, core: 2. Of those that a mesh axis runs over, the one named last changes fastest.
Arguments:
- hidden: bfloat16 [4096, 8192], P('seq'), may hold values from -6 to 6
- w_query: bfloat16 [8192, 4096], P('seq', 'head'), may hold values from -0.0625 to 0.0625
- w_key: bfloat16 [8192, 4096], P('seq', 'head'), may hold values from -0.0625 to 0.0625
- w_value: bfloat16 [8192, 4096], P('seq', 'head'), may hold values from -0.0625 to 0.0625
- cotangent: bfloat16 [4096, 4096], P('seq', 'head'), may hold values from -6 to 6
Outputs:
- step_direction: float32 [4096, 8192], P(('seq', 'head'))
The draws below stay inside these ranges and needn't reach their ends.
All inputs are finite; a program needn't handle non-finite values.
Results may differ from the reference program's by a relative error of at most 0.015.
Values may be sent and summed in bfloat16 or wider, within the bound.
A program may use at most 192 MiB of HBM per device.

```python
import jax
import jax.numpy as jnp
from jax import lax

D = 8192
HEADS = 32
DH = 128
TOK_DEV = 512
TOKENS = 4096
N_HEAD = 4


def levels(key, extent, cuts, smallest, top_value):
    loudness = 1.0
    for dim, blocks in cuts:
        heights = jax.random.uniform(jax.random.fold_in(jax.random.fold_in(key, 6), dim), (blocks,), jnp.float32, smallest / len(cuts), top_value / len(cuts))
        loudness = loudness * jnp.repeat(jnp.exp(heights), extent[dim] // blocks).reshape((-1,) + (1,) * (len(extent) - 1 - dim))
    return loudness


def scatter_about(key, dims, spread, reach, split=(), dtype=jnp.bfloat16):
    drawn = spread * jax.random.normal(key, dims, jnp.float32)
    if split:
        drawn = drawn * levels(key, dims, split, -0.22, 0.18)
    return jnp.clip(drawn, -reach, reach).astype(dtype)


def setup_inputs(seed: int = 0) -> dict:
    keys = jax.random.split(jax.random.key(seed), 6)
    hidden = scatter_about(keys[0], (TOKENS, D), 1.0, 6.0, ((0, 8),))
    w_query = scatter_about(keys[1], (D, HEADS * DH), D ** -0.5, 0.0625, ((0, 8), (1, 4)))
    w_key = scatter_about(keys[2], (D, HEADS * DH), D ** -0.5, 0.0625, ((0, 8), (1, 4)))
    w_value = scatter_about(keys[3], (D, HEADS * DH), D ** -0.5, 0.0625, ((0, 8), (1, 4)))
    cotangent = scatter_about(keys[4], (TOKENS, HEADS * DH), 1.0, 6.0, ((0, 8), (1, 4)))
    return dict(hidden=hidden, w_query=w_query, w_key=w_key, w_value=w_value, cotangent=cotangent)


NORM_EPS = 1e-05
STEP_EPS = 1e-06

def silu_slope(preact):
    sigmoid = jax.nn.sigmoid(preact)
    return sigmoid * (1.0 + preact * (1.0 - sigmoid))

def reference(hidden, w_query, w_key, w_value, cotangent):
    col_total = w_query.shape[1]
    head_count = col_total // DH
    block_count = TOKENS // TOK_DEV
    pre_query = jnp.dot(hidden, w_query, preferred_element_type=jnp.float32)
    pre_key = jnp.dot(hidden, w_key, preferred_element_type=jnp.float32)
    pre_value = jnp.dot(hidden, w_value, preferred_element_type=jnp.float32)

    def blocked(matrix):
        return matrix.reshape(block_count, TOK_DEV, head_count, DH)
    query_rows = blocked(jax.nn.silu(pre_query).astype(jnp.bfloat16))
    key_rows = blocked(jax.nn.silu(pre_key).astype(jnp.bfloat16))
    value_rows = blocked(pre_value.astype(jnp.bfloat16))
    causal = (lax.broadcasted_iota(jnp.int32, (TOK_DEV, TOK_DEV), 0) >= lax.broadcasted_iota(jnp.int32, (TOK_DEV, TOK_DEV), 1))[None]

    def outer_sum(pair):
        return jnp.einsum('thi,thj->hij', pair[0].astype(jnp.float32), pair[1].astype(jnp.float32))
    own_states = lax.map(outer_sum, (key_rows, value_rows))
    zero_state = jnp.zeros_like(own_states[:1])
    before_all = jnp.concatenate([zero_state, jnp.cumsum(own_states, axis=0)[:-1]], axis=0)

    def block_scores(queries, keyed):
        scores = jnp.einsum('thd,shd->hts', queries.astype(jnp.float32), keyed.astype(jnp.float32))
        return jnp.where(causal, scores, 0.0).astype(jnp.bfloat16)

    def forward_block(parts):
        queries, keyed, valued, before = parts
        score_rows = block_scores(queries, keyed)
        inside = jnp.einsum('hts,shd->thd', score_rows.astype(jnp.float32), valued.astype(jnp.float32))
        carried = jnp.einsum('thi,hij->thj', queries.astype(jnp.float32), before, precision=lax.Precision.HIGHEST)
        return inside + carried
    attended = lax.map(forward_block, (query_rows, key_rows, value_rows, before_all))
    scale = lax.rsqrt(lax.optimization_barrier(jnp.mean(attended * attended, axis=-1, keepdims=True)) + NORM_EPS)
    normed = attended * scale
    upstream = blocked(cotangent.astype(jnp.float32))
    grad_att = (scale * (upstream - normed * lax.optimization_barrier(jnp.mean(upstream * normed, axis=-1, keepdims=True)))).astype(jnp.bfloat16)
    own_grads = lax.map(outer_sum, (query_rows, grad_att))
    inclusive = jnp.flip(jnp.cumsum(jnp.flip(own_grads, 0), axis=0), 0)
    after_all = jnp.concatenate([inclusive[1:], zero_state], axis=0)

    def backward_block(parts):
        queries, keyed, valued, grads, before, later_sum = parts
        score_rows = block_scores(queries, keyed).astype(jnp.float32)
        grad_scores = jnp.einsum('thd,shd->hts', grads.astype(jnp.float32), valued.astype(jnp.float32))
        grad_scores = jnp.where(causal, grad_scores, 0.0).astype(jnp.bfloat16).astype(jnp.float32)
        grad_query = jnp.einsum('hts,shd->thd', grad_scores, keyed.astype(jnp.float32)) + jnp.einsum('thj,hij->thi', grads.astype(jnp.float32), before, precision=lax.Precision.HIGHEST)
        grad_key = jnp.einsum('hts,thd->shd', grad_scores, queries.astype(jnp.float32)) + jnp.einsum('thj,hij->thi', valued.astype(jnp.float32), later_sum, precision=lax.Precision.HIGHEST)
        grad_value = jnp.einsum('hts,thd->shd', score_rows, grads.astype(jnp.float32)) + jnp.einsum('thi,hij->thj', keyed.astype(jnp.float32), later_sum, precision=lax.Precision.HIGHEST)
        return (grad_query, grad_key, grad_value)
    grad_query, grad_key, grad_value = lax.map(backward_block, (query_rows, key_rows, value_rows, grad_att, before_all, after_all))
    back_query = (grad_query.reshape(TOKENS, col_total) * silu_slope(pre_query)).astype(jnp.bfloat16)
    back_key = (grad_key.reshape(TOKENS, col_total) * silu_slope(pre_key)).astype(jnp.bfloat16)
    back_value = grad_value.reshape(TOKENS, col_total).astype(jnp.bfloat16)
    group_width = col_total // N_HEAD
    contract = (((1,), (1,)), ((), ()))
    input_grad = jnp.zeros((TOKENS, w_query.shape[0]), jnp.float32)
    for column_group in range(N_HEAD):
        columns = slice(column_group * group_width, (column_group + 1) * group_width)
        partial_value = lax.dot_general(back_query[:, columns], w_query[:, columns], contract, preferred_element_type=jnp.float32)
        partial_value = partial_value + lax.dot_general(back_key[:, columns], w_key[:, columns], contract, preferred_element_type=jnp.float32)
        partial_value = partial_value + lax.dot_general(back_value[:, columns], w_value[:, columns], contract, preferred_element_type=jnp.float32)
        rounded = lax.optimization_barrier(partial_value.astype(jnp.bfloat16))
        input_grad = input_grad + rounded.astype(jnp.float32)
    factor = lax.rsqrt(lax.optimization_barrier(jnp.mean(input_grad * input_grad, axis=-1, keepdims=True)) + STEP_EPS)
    return jnp.tanh(input_grad * factor)
```

```python
import jax
import jax.numpy as jnp
from jax import lax
from jax.sharding import PartitionSpec as P


DH = 128


NORM_EPS = 1e-05
STEP_EPS = 1e-06


F32 = jnp.float32
BF16 = jnp.bfloat16


def silu_slope(preact):
    sigmoid = jax.nn.sigmoid(preact)
    return sigmoid * (1.0 + preact * (1.0 - sigmoid))


def swap(value, axis, mask, size):
    return lax.ppermute(value, axis, [(i, i ^ mask) for i in range(size)])


def scan_states(own, seq_count, later):
    seat = lax.axis_index("seq")
    total = own
    outside = jnp.zeros_like(own)
    mask = 1
    while mask < seq_count:
        other = swap(total.astype(BF16), "seq", mask, seq_count).astype(F32)
        wanted = (seat & mask) == (0 if later else mask)
        outside = outside + jnp.where(wanted, other, 0.0)
        total = total + other
        mask *= 2
    return outside


def on_device(seq_count, head_parts, hidden, w_query, w_key, w_value, cotangent):
    tok_rows, width = hidden.shape
    row_block, col_width = w_query.shape
    head_count = col_width // DH
    seat = lax.axis_index("seq")
    lane = lax.axis_index("head")
    top, pair = seq_count // 2, seq_count // 4
    low_masks = []
    mask = 1
    while mask < pair:
        low_masks.append(mask)
        mask *= 2
    bit = (seat // pair) % 2
    partner = seat ^ pair

    half_width = width // 2
    strip = pair * row_block

    def half_of(array, which):
        return jnp.concatenate(
            [
                lax.dynamic_slice_in_dim(array, side * half_width + which * strip, strip, 1)
                for side in range(2)
            ],
            axis=1,
        )

    core = lane % 2
    half_rows = tok_rows // 2
    sent_rows = lax.dynamic_slice_in_dim(hidden, core * half_rows, half_rows, 0)
    first_rows = swap(half_of(sent_rows, 1 - bit), "seq", pair, seq_count)
    other_rows = swap(first_rows, "head", 1, head_parts)
    lower = jnp.where(core == 0, first_rows, other_rows)
    upper = jnp.where(core == 0, other_rows, first_rows)
    tokens = jnp.concatenate([half_of(hidden, bit), lower, upper], axis=0)

    def gather(weight, cuts):
        step = row_block // cuts
        near = [(0, 0, weight)]
        far = []
        for cut in range(cuts):
            sent = weight[cut * step : (cut + 1) * step]
            far.append((top, cut * step, swap(sent, "seq", top, seq_count)))
        for low in low_masks:
            near = near + [(m ^ low, at, swap(w, "seq", low, seq_count)) for m, at, w in near]
            for m, at, w in tuple(far):
                far.append((m ^ low, at, swap(w, "seq", low, seq_count)))
        return near + far

    key_pieces = gather(w_key, 1)
    value_pieces = gather(w_value, 1)
    query_pieces = gather(w_query, 2)

    def project(pieces):
        acc = None
        for m, at, rows in pieces:
            block = seat ^ m
            column = ((block // top) * pair + block % pair) * row_block + at
            term = jnp.dot(
                lax.dynamic_slice_in_dim(tokens, column, rows.shape[0], 1),
                rows,
                preferred_element_type=F32,
            )
            acc = term if acc is None else acc + term
        theirs = swap(acc[tok_rows:].astype(BF16), "seq", pair, seq_count)
        return acc[:tok_rows] + theirs.astype(F32)

    pre_key = project(key_pieces)
    pre_value = project(value_pieces)
    pre_query = project(query_pieces)

    key_rows = jax.nn.silu(pre_key).astype(BF16).reshape(tok_rows, head_count, DH)
    value_rows = pre_value.astype(BF16).reshape(tok_rows, head_count, DH)
    own_state = jnp.einsum("thi,thj->hij", key_rows, value_rows, preferred_element_type=F32)
    before = scan_states(own_state, seq_count, False)
    query_rows = jax.nn.silu(pre_query).astype(BF16).reshape(tok_rows, head_count, DH)
    causal = (
        lax.broadcasted_iota(jnp.int32, (tok_rows, tok_rows), 0)
        >= lax.broadcasted_iota(jnp.int32, (tok_rows, tok_rows), 1)
    )[None]
    scores = jnp.einsum("thd,shd->hts", query_rows, key_rows, preferred_element_type=F32)
    score_rows = jnp.where(causal, scores, 0.0).astype(BF16)
    inside = jnp.einsum("hts,shd->thd", score_rows, value_rows, preferred_element_type=F32)
    carried = jnp.einsum(
        "thi,hij->thj", query_rows.astype(F32), before, precision=lax.Precision.HIGHEST
    )
    attended = inside + carried
    scale = lax.rsqrt(jnp.mean(attended * attended, axis=-1, keepdims=True) + NORM_EPS)
    normed = attended * scale
    upstream = cotangent.astype(F32).reshape(tok_rows, head_count, DH)
    grad_att = (
        scale * (upstream - normed * jnp.mean(upstream * normed, axis=-1, keepdims=True))
    ).astype(BF16)
    own_grad = jnp.einsum("thi,thj->hij", query_rows, grad_att, preferred_element_type=F32)
    later_sum = scan_states(own_grad, seq_count, True)
    grad_scores = jnp.einsum("thd,shd->hts", grad_att, value_rows, preferred_element_type=F32)
    grad_scores = jnp.where(causal, grad_scores, 0.0).astype(BF16)
    grad_query = jnp.einsum(
        "hts,shd->thd", grad_scores, key_rows, preferred_element_type=F32
    ) + jnp.einsum("thj,hij->thi", grad_att.astype(F32), before, precision=lax.Precision.HIGHEST)
    grad_key = jnp.einsum(
        "hts,thd->shd", grad_scores, query_rows, preferred_element_type=F32
    ) + jnp.einsum(
        "thj,hij->thi", value_rows.astype(F32), later_sum, precision=lax.Precision.HIGHEST
    )
    grad_value = jnp.einsum(
        "hts,thd->shd", score_rows, grad_att, preferred_element_type=F32
    ) + jnp.einsum(
        "thi,hij->thj", key_rows.astype(F32), later_sum, precision=lax.Precision.HIGHEST
    )
    back_query = (grad_query.reshape(tok_rows, col_width) * silu_slope(pre_query)).astype(BF16)
    back_key = (grad_key.reshape(tok_rows, col_width) * silu_slope(pre_key)).astype(BF16)
    back_value = grad_value.reshape(tok_rows, col_width).astype(BF16)

    def both(back):
        return jnp.concatenate([back, swap(back, "seq", pair, seq_count)], axis=0)

    backs = both(back_query), both(back_key), both(back_value)
    contract = (((1,), (1,)), ((), ()))
    out_rows = tok_rows // head_parts
    input_grad = jnp.zeros((out_rows, width), F32)
    whole_query = query_pieces[: len(query_pieces) // 3]
    for place in range(len(whole_query), len(query_pieces), 2):
        m, _, rows = query_pieces[place]
        rows = jnp.concatenate([rows, query_pieces[place + 1][2]], axis=0)
        whole_query = whole_query + [(m, 0, rows)]
    for place in range(len(key_pieces)):
        m, at, _ = key_pieces[place]
        part = None
        for back, pieces in zip(backs, (whole_query, key_pieces, value_pieces)):
            term = lax.dot_general(back, pieces[place][2], contract, preferred_element_type=F32)
            part = term if part is None else part + term
        columns = part.shape[1]
        part = part.reshape(2, head_parts, out_rows, columns)
        mask = 1
        while mask < head_parts:
            groups = part.reshape(2, part.shape[1] // 2, 2, out_rows, columns)
            side = (lane // mask) % 2
            kept = lax.dynamic_index_in_dim(groups, side, 2, keepdims=False)
            sent = lax.dynamic_index_in_dim(groups, 1 - side, 2, keepdims=False)
            got = swap(sent.astype(BF16), "head", mask, head_parts)
            part = kept + got.astype(F32)
            mask *= 2
        mine, theirs = part[0, 0], part[1, 0]
        fetched = swap(theirs.astype(BF16), "seq", pair, seq_count).astype(F32)
        input_grad = lax.dynamic_update_slice(input_grad, mine, (0, (seat ^ m) * row_block + at))
        input_grad = lax.dynamic_update_slice(
            input_grad, fetched, (0, (partner ^ m) * row_block + at)
        )
    factor = lax.rsqrt(jnp.mean(input_grad * input_grad, axis=-1, keepdims=True) + STEP_EPS)
    return jnp.tanh(input_grad * factor)


def solution(mesh):
    def body(*args):
        return on_device(mesh.shape["seq"], mesh.shape["head"], *args)

    return jax.shard_map(
        body,
        mesh=mesh,
        in_specs=(
            P("seq", None),
            P("seq", "head"),
            P("seq", "head"),
            P("seq", "head"),
            P("seq", "head"),
        ),
        out_specs=P(("seq", "head"), None),
        check_vma=False,
    )
```
